32 devices in a mesh: sector: 8 (over y, x, core), op: 4 (over z).
Axes of the slice: x: 2, y: 2, z: 4, core: 2. Of those that a mesh axis runs over, the one named last changes fastest.
Arguments:
- wavefunction: bfloat16 [8, 768, 1536], P('sector', 'op'), may hold values from -6 to 6
- basis: bfloat16 [8, 1536, 768], P('sector'), may hold values from -0.15625 to 0.15625
- left_ops: bfloat16 [20, 768, 768], P('op'), may hold values from -0.046875 to 0.046875
- right_ops: bfloat16 [20, 768, 768], P('op'), may hold values from -0.21875 to 0.21875
- offsets: int32 [20], P('op'), may hold values from -2 to 2, as said below
- sector_sizes: int32 [8], P('sector'), may hold values from 384 to 1536
Outputs:
- evolved: bfloat16 [8, 768, 1536], P('sector', 'op')
The draws below stay inside these ranges and needn't reach their ends.
Inputs may be any that keep to these rules, and one draw needn't show every extreme that they name: Every value from -2 to 2 occurs among the 20 offsets, any two of them equally often up to one. Only the first sector_sizes[s] left states of sector s are live.
All inputs are finite; a program needn't handle non-finite values.
Results may differ from the reference program's by a relative error of at most 0.014.
Values may be sent and summed in bfloat16 or wider, within the bound.
No kernel may reach another device: no remote copies, remote signals or barrier semaphores. Data moves between devices by JAX's collectives and lax.ppermute only.
A program may use at most 128 MiB of HBM per device.

```python
import jax
import jax.numpy as jnp
from jax import lax

BOND = 768
LEFT = 1536
REACH = 2
STEPS = 2
SECTORS = 8
PAIRS = 20


def draw_offsets(key, part):
    ordering = jax.random.permutation(jax.random.fold_in(key, 11), PAIRS)
    return (ordering % (2 * REACH + 1) - REACH).astype(jnp.int32)


def with_ends(array, rng, low, high):
    dims = array.shape
    place = [jax.random.randint(jax.random.fold_in(rng, axis), (), 0, dims[axis]) for axis in range(len(dims))]
    array = array.at[tuple(place)].set(low)
    longest = dims.index(max(dims))
    place[longest] = (place[longest] + 1) % dims[longest]
    return array.at[tuple(place)].set(high)


def block_scale(key, shape, shards, least, high):
    factor_of, own = 1.0, jax.random.fold_in(key, 6)
    for dim, shards_of in shards:
        steps = jnp.exp(jax.random.uniform(jax.random.fold_in(own, dim), (shards_of,), jnp.float32, least / len(shards), high / len(shards)))
        factor_of = factor_of * jnp.repeat(steps, shape[dim] // shards_of).reshape([-1 if axis == dim else 1 for axis in range(len(shape))])
    return factor_of


def centred(stream_key, shape, scale, most, split=(), held_as=jnp.bfloat16):
    entries = jax.random.normal(stream_key, shape, jnp.float32) * scale
    if len(split) > 0:
        entries = block_scale(stream_key, shape, split, -0.22, 0.18) * entries
    return jnp.clip(entries, min=-most, max=most).astype(held_as)


def setup_inputs(seed: int = 0) -> dict:
    streams_of = jax.random.split(jax.random.key(seed), 7)
    wavefunction = centred(streams_of[0], (SECTORS, BOND, LEFT), 1.0, 6.0, ((0, 8), (1, 4)))
    basis = centred(streams_of[1], (SECTORS, LEFT, BOND), LEFT ** -0.5, 0.15625, ((0, 8),))
    left_ops = centred(streams_of[2], (PAIRS, BOND, BOND), (BOND * PAIRS) ** -0.5, 0.046875, ((0, 4),))
    right_ops = centred(streams_of[3], (PAIRS, BOND, BOND), BOND ** -0.5, 0.21875, ((0, 4),))
    offsets = draw_offsets(jax.random.fold_in(streams_of[6], 71), 0)
    sector_sizes = with_ends(jax.random.randint(streams_of[5], (SECTORS,), LEFT // 4, LEFT + 1), jax.random.fold_in(streams_of[5], 1), LEFT // 4, LEFT).astype(jnp.int32)
    return {"wavefunction": wavefunction, "basis": basis, "left_ops": left_ops, "right_ops": right_ops, "offsets": offsets, "sector_sizes": sector_sizes}


increment_width = 0.75


def reference(wavefunction, basis, left_ops, right_ops, offsets, sector_sizes):
    sector_count = wavefunction.shape[0]
    column_entries = jnp.arange(wavefunction.shape[2], dtype=jnp.int32)
    live_mask = column_entries[None, :] < sector_sizes[:, None]
    current = jnp.where(live_mask[:, None, :], wavefunction, jnp.zeros_like(wavefunction))
    masked_basis = jnp.where(live_mask[:, :, None], basis, jnp.zeros_like(basis))
    sector_ids = jnp.arange(sector_count, dtype=jnp.int32)
    left_wide = left_ops.astype(jnp.float32)
    broad_east_factor = right_ops.astype(jnp.float32)
    enlarged_state_space = masked_basis.astype(jnp.float32)
    for repeat in range(STEPS):
        transformed_blocks = jnp.einsum("sbl,slc->sbc", current.astype(jnp.float32), enlarged_state_space).astype(jnp.bfloat16)
        transformed_blocks = lax.optimization_barrier(transformed_blocks)

        def single_sector(sector_index):
            targets = (sector_index + offsets).astype(jnp.int32)
            inside_range = (targets >= 0) & (targets < sector_count)
            guarded_destinations = jnp.clip(targets, 0, sector_count - 1).astype(jnp.int32)
            chosen_tiles = transformed_blocks[guarded_destinations]
            chosen_tiles = jnp.where(inside_range[:, None, None], chosen_tiles, jnp.zeros_like(chosen_tiles))
            half_product = jnp.einsum("kab,kbc->kac", left_wide, chosen_tiles.astype(jnp.float32)).astype(jnp.bfloat16)
            half_product = lax.optimization_barrier(half_product)
            return jnp.einsum("kac,kdc->ad", half_product.astype(jnp.float32), broad_east_factor)

        overall_tile_count = lax.map(single_sector, sector_ids).astype(jnp.bfloat16)
        overall_tile_count = lax.optimization_barrier(overall_tile_count)
        lifted_tiles = jnp.einsum("zqt,zit->zqi", overall_tile_count.astype(jnp.float32), enlarged_state_space)
        current = (current.astype(jnp.float32) - increment_width * lifted_tiles).astype(jnp.bfloat16)
    return current
```

```python
import functools

import jax
import jax.numpy as jnp
from jax import lax
from jax.experimental import pallas as pl
from jax.experimental.pallas import tpu as pltpu
from jax.sharding import PartitionSpec as P

REACH = 2
STEPS = 2

increment_width = 0.75


def column_chunks(width):
    if width % 768 == 0:
        first = width // 3 * 2
        return [(0, first), (first, width - first)]
    return [(0, width)]


def places(sectors):
    if sectors == 8:
        return [0, 1, 2, 3, 6, 7, 4, 5]
    return list(range(sectors))


def gather_rows(block, position, peers):
    if peers != 4:
        return lax.all_gather(block, "op", axis=0, tiled=True)
    pair = [(i, i ^ 1) for i in range(4)]
    mirror = [(i, 3 - i) for i in range(4)]
    far = lax.ppermute(block, "op", mirror)
    near = lax.ppermute(block, "op", pair)
    cross = lax.ppermute(far, "op", pair)
    held = [block, near, cross, far]
    odd = (position & 1) == 1
    upper = (position & 2) == 2
    held = [jnp.where(odd, held[i ^ 1], held[i]) for i in range(4)]
    held = [jnp.where(upper, held[i ^ 2], held[i]) for i in range(4)]
    return jnp.concatenate(held, axis=0)


def pair_kernel(first, last, start, peers, where_ref, offs_ref, left_ref, right_ref, *refs):
    sources = refs[: 2 * REACH + 1]
    refs = refs[2 * REACH + 1 :]
    if not first:
        before, refs = refs[0], refs[1:]
    outs, total = refs[:-1], refs[-1]
    size = sources[0].shape[1]
    if first:
        total[...] = jnp.zeros_like(total)
    else:
        total[...] = before[...]

    def one(k, carry):
        for d, source in enumerate(sources):

            @pl.when(offs_ref[k] == d - REACH)
            def _():
                half = jnp.dot(
                    left_ref[k], source[...], preferred_element_type=jnp.float32
                ).astype(jnp.bfloat16)
                total[...] += lax.dot_general(
                    half,
                    right_ref[k, :, start : start + size],
                    (((1,), (1,)), ((), ())),
                    preferred_element_type=jnp.float32,
                )

        return carry

    lax.fori_loop(0, left_ref.shape[0], one, 0)
    if not last:
        outs[0][...] = total[...]
        return
    rows = outs[0].shape[0]
    for i, out in enumerate(outs):
        block = where_ref[0] ^ i if peers == 4 else i
        out[...] = total[pl.ds(pl.multiple_of(block * rows, rows), rows), :].astype(out.dtype)


def pair_products(position, offs, left, right, sources, before, start, last, peers):
    pairs, bond, _ = left.shape
    size = sources[0].shape[1]
    first = before is None
    vmem = pl.BlockSpec(memory_space=pltpu.VMEM)
    smem = pl.BlockSpec(memory_space=pltpu.SMEM)
    operands = [left, right, *sources] + ([] if first else [before])
    if last:
        out_shape = [jax.ShapeDtypeStruct((bond // peers, bond), jnp.bfloat16)] * peers
    else:
        out_shape = [jax.ShapeDtypeStruct((bond, bond), jnp.float32)]
    return pl.pallas_call(
        functools.partial(pair_kernel, first, last, start, peers),
        in_specs=[smem, smem] + [vmem] * len(operands),
        out_specs=[vmem] * len(out_shape),
        out_shape=out_shape,
        scratch_shapes=[pltpu.VMEM((bond, bond), jnp.float32)],
        compiler_params=pltpu.CompilerParams(vmem_limit_bytes=32 * 1024 * 1024),
        cost_estimate=pl.CostEstimate(
            flops=4 * pairs * bond * bond * size,
            bytes_accessed=4 * pairs * bond * bond,
            transcendentals=0,
        ),
    )(position, offs, *operands)


def scatter_sum(parts, peers):
    if peers != 4:
        return lax.psum_scatter(
            jnp.concatenate(parts, axis=0), "op", scatter_dimension=0, tiled=True
        ).astype(jnp.float32)
    pair = [(i, i ^ 1) for i in range(4)]
    mirror = [(i, 3 - i) for i in range(4)]
    wide = [p.astype(jnp.float32) for p in parts]
    passed = lax.ppermute(parts[2], "op", pair)
    near = lax.ppermute(parts[1], "op", pair)
    joined = (wide[3] + passed.astype(jnp.float32)).astype(jnp.bfloat16)
    far = lax.ppermute(joined, "op", mirror)
    return wide[0] + near.astype(jnp.float32) + far.astype(jnp.float32)


def on_device(wavefunction, basis, left_ops, right_ops, offsets, sector_sizes):
    sectors = lax.axis_size("sector")
    peers = lax.axis_size("op")
    position = lax.axis_index("op")
    core = lax.axis_index("sector") & 1
    place = places(sectors)
    inside = [i for i in range(sectors)]
    move = [(i, place[i]) for i in inside]
    swap = [(i, i ^ 1) for i in inside]
    outer = [(place[i], place[j]) for j in inside for i in [j + 2 if j % 2 == 0 else j - 2] if i in inside]
    inner = [(place[i], place[j]) for j in inside for i in [j - 2 if j % 2 == 0 else j + 2] if i in inside]
    turned = jnp.where(core == 0, offsets, -offsets)
    where = position.reshape(1).astype(jnp.int32)

    live = sector_sizes[0]
    columns = lax.broadcasted_iota(jnp.int32, wavefunction.shape, 2)
    current = jnp.where(columns < live, wavefunction, jnp.zeros_like(wavefunction))[0]
    rows = lax.broadcasted_iota(jnp.int32, basis.shape, 1)
    masked_basis = jnp.where(rows < live, basis, jnp.zeros_like(basis))[0]
    chunks = column_chunks(basis.shape[2])
    for _ in range(STEPS):
        total = None
        for number, (start, size) in enumerate(chunks):
            rotated = jnp.dot(
                current,
                masked_basis[:, start : start + size],
                preferred_element_type=jnp.float32,
            ).astype(jnp.bfloat16)
            if place != inside:
                rotated = lax.ppermute(rotated, "sector", move)
            own = gather_rows(rotated, position, peers)
            above = lax.ppermute(own, "sector", outer)
            below = lax.ppermute(own, "sector", inner)
            partner = lax.ppermute(own, "sector", swap)
            across = lax.ppermute(above, "sector", swap)
            sources = [below, across, own, partner, above]
            last = number == len(chunks) - 1
            parts = pair_products(
                where, turned, left_ops, right_ops, sources, total, start, last, peers
            )
            total = parts[0]
        summed = scatter_sum(parts, peers).astype(jnp.bfloat16)
        if place != inside:
            summed = lax.ppermute(summed, "sector", move)
        lifted = jnp.einsum(
            "ad,ld->al", summed, masked_basis, preferred_element_type=jnp.float32
        )
        current = (current.astype(jnp.float32) - increment_width * lifted).astype(jnp.bfloat16)
    return current[None]


def solution(mesh):
    return jax.shard_map(
        on_device,
        mesh=mesh,
        in_specs=(
            P("sector", "op", None),
            P("sector", None, None),
            P("op", None, None),
            P("op", None, None),
            P("op"),
            P("sector"),
        ),
        out_specs=P("sector", "op", None),
        check_vma=False,
    )
```

```python
import functools

import jax
import jax.numpy as jnp
from jax import lax
from jax.experimental import pallas as pl
from jax.experimental.pallas import tpu as pltpu
from jax.sharding import PartitionSpec as P


REACH = 2
STEPS = 2

increment_width = 0.75


def column_chunks(width):
    if width % 768 == 0:
        first = width // 3 * 2
        return [(0, first), (first, width - first)]
    return [(0, width)]


def places(sectors):
    if sectors == 8:
        return [0, 1, 2, 3, 6, 7, 4, 5]
    return list(range(sectors))


def gather_rows(block, position, peers):
    if peers != 4:
        return lax.all_gather(block, "op", axis=0, tiled=True)
    pair = [(i, i ^ 1) for i in range(4)]
    mirror = [(i, 3 - i) for i in range(4)]
    far = lax.ppermute(block, "op", mirror)
    near = lax.ppermute(block, "op", pair)
    cross = lax.ppermute(far, "op", pair)
    held = [block, near, cross, far]
    odd = (position & 1) == 1
    upper = (position & 2) == 2
    held = [jnp.where(odd, held[i ^ 1], held[i]) for i in range(4)]
    held = [jnp.where(upper, held[i ^ 2], held[i]) for i in range(4)]
    return jnp.concatenate(held, axis=0)


def pair_kernel(first, last, peers, where_ref, offs_ref, left_ref, right_ref, *refs):
    sources = refs[: 2 * REACH + 1]
    refs = refs[2 * REACH + 1 :]
    if not first:
        before, refs = refs[0], refs[1:]
    outs, (halves, total) = refs[:-2], refs[-2:]
    size = sources[0].shape[1]

    def one(k, carry):
        for d, source in enumerate(sources):

            @pl.when(offs_ref[k] == d - REACH)
            def _():
                halves[:, pl.ds(pl.multiple_of(k * size, size), size)] = jnp.dot(
                    left_ref[k], source[...], preferred_element_type=jnp.float32
                ).astype(jnp.bfloat16)

        return carry

    lax.fori_loop(0, left_ref.shape[0], one, 0)
    product = lax.dot_general(
        halves[...], right_ref[...], (((1,), (1,)), ((), ())), preferred_element_type=jnp.float32
    )
    if not first:
        product = before[...] + product
    if not last:
        outs[0][...] = product
        return
    total[...] = product
    rows = outs[0].shape[0]
    for i, out in enumerate(outs):
        block = where_ref[0] ^ i if peers == 4 else i
        out[...] = total[pl.ds(pl.multiple_of(block * rows, rows), rows), :].astype(out.dtype)


def pair_products(position, offs, left, right, sources, before, last, peers):
    pairs, bond, _ = left.shape
    size = sources[0].shape[1]
    first = before is None
    vmem = pl.BlockSpec(memory_space=pltpu.VMEM)
    smem = pl.BlockSpec(memory_space=pltpu.SMEM)
    operands = [left, right, *sources] + ([] if first else [before])
    if last:
        out_shape = [jax.ShapeDtypeStruct((bond // peers, bond), jnp.bfloat16)] * peers
    else:
        out_shape = [jax.ShapeDtypeStruct((bond, bond), jnp.float32)]
    return pl.pallas_call(
        functools.partial(pair_kernel, first, last, peers),
        in_specs=[smem, smem] + [vmem] * len(operands),
        out_specs=[vmem] * len(out_shape),
        out_shape=out_shape,
        scratch_shapes=[
            pltpu.VMEM((bond, pairs * size), jnp.bfloat16),
            pltpu.VMEM((bond, bond) if last else (8, 128), jnp.float32),
        ],
        compiler_params=pltpu.CompilerParams(vmem_limit_bytes=12 * 1024 * 1024),
        cost_estimate=pl.CostEstimate(
            flops=4 * pairs * bond * bond * size,
            bytes_accessed=4 * pairs * bond * bond,
            transcendentals=0,
        ),
    )(position, offs, *operands)


def scatter_sum(parts, peers):
    if peers != 4:
        return lax.psum_scatter(
            jnp.concatenate(parts, axis=0), "op", scatter_dimension=0, tiled=True
        ).astype(jnp.float32)
    pair = [(i, i ^ 1) for i in range(4)]
    mirror = [(i, 3 - i) for i in range(4)]
    wide = [p.astype(jnp.float32) for p in parts]
    passed = lax.ppermute(parts[2], "op", pair)
    near = lax.ppermute(parts[1], "op", pair)
    joined = (wide[3] + passed.astype(jnp.float32)).astype(jnp.bfloat16)
    far = lax.ppermute(joined, "op", mirror)
    return wide[0] + near.astype(jnp.float32) + far.astype(jnp.float32)


def prepare_kernel(chunks, left_ref, right_ref, left_out, *refs):
    outs, sems = refs[:-1], refs[-1]
    copies = []
    for k in range(left_ref.shape[0]):
        copies.append((left_ref.at[k], left_out.at[k]))
        for (start, size), out in zip(chunks, outs):
            copies.append(
                (right_ref.at[k, :, start : start + size], out.at[:, k * size : (k + 1) * size])
            )
    copies = [pltpu.make_async_copy(a, b, sems.at[n]) for n, (a, b) in enumerate(copies)]
    for copy in copies:
        copy.start()
    for copy in copies:
        copy.wait()


def prepare(left, right, chunks):
    pairs, bond, _ = right.shape
    vmem = pl.BlockSpec(memory_space=pltpu.VMEM)
    hbm = pl.BlockSpec(memory_space=pl.ANY)
    out_shape = [jax.ShapeDtypeStruct(left.shape, left.dtype)] + [
        jax.ShapeDtypeStruct((bond, pairs * size), right.dtype) for _, size in chunks
    ]
    return pl.pallas_call(
        functools.partial(prepare_kernel, chunks),
        in_specs=[hbm, hbm],
        out_specs=[vmem] * len(out_shape),
        out_shape=out_shape,
        scratch_shapes=[pltpu.SemaphoreType.DMA((pairs * len(out_shape),))],
        compiler_params=pltpu.CompilerParams(vmem_limit_bytes=2 * 1024 * 1024),
        cost_estimate=pl.CostEstimate(
            flops=0, bytes_accessed=4 * (left.size + right.size), transcendentals=0
        ),
    )(left, right)


def on_device(wavefunction, basis, left_ops, right_ops, offsets, sector_sizes):
    sectors = lax.axis_size("sector")
    peers = lax.axis_size("op")
    position = lax.axis_index("op")
    core = lax.axis_index("sector") & 1
    place = places(sectors)
    inside = [i for i in range(sectors)]
    moves = place != inside
    move = [(i, place[i]) for i in inside]
    swap = [(i, i ^ 1) for i in inside]
    outer = [(place[i], place[j]) for j in inside for i in [j + 2 if j % 2 == 0 else j - 2] if i in inside]
    inner = [(place[i], place[j]) for j in inside for i in [j - 2 if j % 2 == 0 else j + 2] if i in inside]
    turned = jnp.where(core == 0, offsets, -offsets)
    where = position.reshape(1).astype(jnp.int32)

    live = sector_sizes[0]
    rows = lax.broadcasted_iota(jnp.int32, basis.shape[1:], 0)
    masked_basis = jnp.where(rows < live, basis[0], jnp.zeros_like(basis[0]))
    columns = lax.broadcasted_iota(jnp.int32, wavefunction.shape[1:], 1)
    current = jnp.where(columns < live, wavefunction[0], jnp.zeros_like(wavefunction[0]))
    chunks = column_chunks(basis.shape[2])
    for step in range(STEPS):
        if step == 0:
            rotated = jnp.dot(current, masked_basis, preferred_element_type=jnp.float32)
            rotated = rotated.astype(jnp.bfloat16)
            pieces = [rotated[:, start : start + size] for start, size in chunks]
            if moves:
                pieces = [lax.ppermute(piece, "sector", move) for piece in pieces]
            rotated = [piece.astype(jnp.float32) for piece in pieces]
            gram = lax.dot_general(
                masked_basis,
                masked_basis,
                (((0,), (0,)), ((), ())),
                preferred_element_type=jnp.float32,
            ).astype(jnp.bfloat16)
            gram, left, right = lax.optimization_barrier((gram, left_ops, right_ops))
            left, *rights = prepare(left, right, chunks)
        else:
            rotated = [
                piece
                - increment_width
                * jnp.dot(
                    summed.astype(jnp.bfloat16),
                    gram[:, start : start + size],
                    preferred_element_type=jnp.float32,
                )
                for piece, (start, size) in zip(rotated, chunks)
            ]
            pieces = [piece.astype(jnp.bfloat16) for piece in rotated]
        total = None
        for number, piece in enumerate(pieces):
            own = gather_rows(piece, position, peers)
            above = lax.ppermute(own, "sector", outer)
            below = lax.ppermute(own, "sector", inner)
            partner = lax.ppermute(own, "sector", swap)
            across = lax.ppermute(above, "sector", swap)
            sources = [below, across, own, partner, above]
            last = number == len(chunks) - 1
            parts = pair_products(where, turned, left, rights[number], sources, total, last, peers)
            total = parts[0]
        summed = scatter_sum(parts, peers)
        if step == 0 and moves:
            gram = lax.ppermute(gram, "sector", move)
        changes = summed if step == 0 else changes + summed
    changes = changes.astype(jnp.bfloat16)
    if moves:
        changes = lax.ppermute(changes, "sector", move)
    lifted = lax.dot_general(
        changes, masked_basis, (((1,), (1,)), ((), ())), preferred_element_type=jnp.float32
    )
    current = (current.astype(jnp.float32) - increment_width * lifted).astype(jnp.bfloat16)
    return current[None]


def solution(mesh):
    return jax.shard_map(
        on_device,
        mesh=mesh,
        in_specs=(
            P("sector", "op", None),
            P("sector", None, None),
            P("op", None, None),
            P("op", None, None),
            P("op"),
            P("sector"),
        ),
        out_specs=P("sector", "op", None),
        check_vma=False,
    )
```
